32 devices in a mesh: batch: 1, seq: 32 (over z, y, x, core).
Axes of the slice: x: 2, y: 2, z: 4, core: 2. Of those that a mesh axis runs over, the one named last changes fastest.
Arguments:
- tokens: bfloat16 [304, 262144], P('batch', 'seq'), may hold values from -6 to 6
- norm_gain: float32 [2, 304], replicated, may hold values from 0.5 to 1.5
- in_weight: bfloat16 [2, 608, 304], replicated, may hold values from -0.3125 to 0.3125
- in_bias: float32 [2, 608], replicated, may hold values from -3 to 3
- out_weight: bfloat16 [2, 304, 608], replicated, may hold values from -0.25 to 0.25
- out_bias: float32 [2, 304], replicated, may hold values from -3 to 3
Outputs:
- mixed: bfloat16 [304, 262144], P('batch', 'seq')
The draws below stay inside these ranges and needn't reach their ends.
All inputs are finite; a program needn't handle non-finite values.
Results may differ from the reference program's by a relative error of at most 0.0056.
Values may be sent and summed in bfloat16 or wider, within the bound.
A program may use at most 64 MiB of HBM per device.

```python
import jax
import jax.numpy as jnp
from jax import lax

TRACK_CH = 16
TRACKS = 19
LENGTH = 262144
BLOCKS = 2
D = 304
HID = 608


def shard_levels(key, extent, split, smallest, largest):
    loudness, own = 1.0, jax.random.fold_in(key, 6)
    for axis_at, shards_of in split:
        heights = jnp.exp(jax.random.uniform(jax.random.fold_in(own, axis_at), (shards_of,), jnp.float32, smallest / len(split), largest / len(split)))
        loudness = loudness * jnp.repeat(heights, extent[axis_at] // shards_of).reshape([-1 if axis == axis_at else 1 for axis in range(len(extent))])
    return loudness


def normal_values(stream_key, extent, deviation, bound, split=(), kind=jnp.bfloat16):
    array = deviation * jax.random.normal(stream_key, extent, jnp.float32)
    if split:
        array = array * shard_levels(stream_key, extent, split, -0.22, 0.18)
    return jnp.clip(array, -bound, bound).astype(kind)


def setup_inputs(seed: int = 0, part: int = 0) -> dict:
    seeds = jax.random.split(jax.random.key(seed), 7)
    part_keys = jax.random.split(jax.random.fold_in(seeds[6], part), 7)
    tokens = normal_values(part_keys[0], (D, LENGTH), 1.0, 6.0, ((1, 32),))
    norm_gain = jnp.clip(jax.random.uniform(seeds[1], (BLOCKS, D), jnp.float32, 0.5, 1.5), 0.5, 1.5)
    in_weight = normal_values(seeds[2], (BLOCKS, HID, D), D ** -0.5, 0.3125)
    in_bias = normal_values(seeds[3], (BLOCKS, HID), 0.5, 3.0, (), jnp.float32)
    out_weight = normal_values(seeds[4], (BLOCKS, D, HID), HID ** -0.5, 0.25)
    out_bias = normal_values(seeds[5], (BLOCKS, D), 0.5, 3.0, (), jnp.float32)
    return dict(tokens=tokens, norm_gain=norm_gain, in_weight=in_weight, in_bias=in_bias, out_weight=out_weight, out_bias=out_bias)


def rotate(current):
    pieces = [current[0:TRACK_CH]]
    for track_no in range(1, TRACKS):
        offset = 2 ** (track_no - 1)
        one_track = current[track_no * TRACK_CH:(track_no + 1) * TRACK_CH]
        pieces.append(jnp.roll(one_track, offset, axis=1))
    return jnp.concatenate(pieces, 0)

def mix_rows(rotated, gain, in_weight, in_bias, out_weight, out_bias):
    as_float = rotated.astype(jnp.float32)
    mean_square = lax.optimization_barrier(jnp.mean(as_float * as_float, axis=0, keepdims=True))
    normed = (as_float * gain[:, None] * lax.rsqrt(mean_square + 1e-06)).astype(jnp.bfloat16)
    pre_act = jnp.dot(in_weight, normed, preferred_element_type=jnp.float32) + in_bias[:, None]
    active = jax.nn.gelu(pre_act, approximate=True).astype(jnp.bfloat16)
    summed = as_float + jnp.dot(out_weight, active, preferred_element_type=jnp.float32) + out_bias[:, None]
    return summed.astype(jnp.bfloat16)

def reference(tokens, norm_gain, in_weight, in_bias, out_weight, out_bias):
    current = tokens
    piece_count = 64
    piece_cols = LENGTH // piece_count
    for block_no in range(BLOCKS):
        rotated = rotate(current)
        stacked = rotated.reshape(D, piece_count, piece_cols).transpose(1, 0, 2)
        result = lax.map(lambda column_block: mix_rows(column_block, norm_gain[block_no], in_weight[block_no], in_bias[block_no], out_weight[block_no], out_bias[block_no]), stacked)
        current = result.transpose(1, 0, 2).reshape(D, LENGTH)
    return current
```

```python
import functools

import jax
import jax.numpy as jnp
from jax import lax
from jax.experimental import pallas as pl
from jax.experimental.pallas import tpu as pltpu
from jax.sharding import PartitionSpec as P

TRACK_CH = 16
TRACKS = 19
BLOCKS = 2
LANES = 128
CHUNK = 1024
TILE = 512
MESH = pl.DeviceIdType.MESH


class Plan:
    def __init__(self, count, rows, chunk, tile):
        self.count, self.rows, self.chunk, self.tile = count, rows, chunk, tile
        self.chunks = rows // chunk
        self.short = 0
        while self.short + 1 < TRACKS and 2**self.short < rows:
            self.short += 1
        self.near = (1 + self.short) * TRACK_CH
        self.distances = [2 ** (t - 1) // rows for t in range(1 + self.short, TRACKS)]
        self.far = len(self.distances)
        self.halo = max(2 ** (self.short - 1), LANES)
        self.pieces = []
        small = sum(1 for t in range(1, 1 + self.short) if 2 ** (t - 1) < LANES)
        self.pieces.append((TRACK_CH, small * TRACK_CH, LANES, LANES, self.chunks - 1, 0))
        for t in range(1 + small, 1 + self.short):
            offset = 2 ** (t - 1)
            width = min(offset, chunk)
            for part in range(offset // width):
                from_end = offset - part * width
                source = (rows - from_end) // chunk
                self.pieces.append((t * TRACK_CH, TRACK_CH, from_end, width, source, part))
        peers = []
        for d in self.distances + [1]:
            for signed in (d, count - d):
                if signed % count and signed % count not in peers:
                    peers.append(signed % count)
        self.peers = peers


def rotated_tile(plan, ext, far, col):
    tile, halo = plan.tile, plan.halo
    parts = []
    for t in range(1 + plan.short):
        rows = pl.ds(t * TRACK_CH, TRACK_CH)
        offset = 0 if t == 0 else 2 ** (t - 1)
        if offset % LANES == 0:
            start = pl.multiple_of(halo - offset + col, LANES)
            parts.append(ext[rows, pl.ds(start, tile)].astype(jnp.float32))
        else:
            start = pl.multiple_of(halo - LANES + col, LANES)
            window = ext[rows, pl.ds(start, tile + LANES)].astype(jnp.float32)
            parts.append(pltpu.roll(window, offset, 1)[:, LANES:])
    parts.append(far[:, pl.ds(pl.multiple_of(col, LANES), tile)].astype(jnp.float32))
    return jnp.concatenate(parts, 0)


def mix_tile(as_float, gain, in_weight, in_bias, out_weight, out_bias):
    mean_square = jnp.mean(as_float * as_float, axis=0, keepdims=True)
    normed = (as_float * gain * lax.rsqrt(mean_square + 1e-06)).astype(jnp.bfloat16)
    pre_act = jnp.dot(in_weight, normed, preferred_element_type=jnp.float32) + in_bias
    inner = pre_act * (0.7978845608028654 + 0.035677408136300125 * (pre_act * pre_act))
    half = 0.5 * pre_act
    active = (half + half * jnp.tanh(inner)).astype(jnp.bfloat16)
    summed = as_float + jnp.dot(out_weight, active, preferred_element_type=jnp.float32) + out_bias
    return summed.astype(jnp.bfloat16)


def kernel(plan, tokens, gain, w_in, b_in, w_out, b_out, out,
           ext0, ext1, far0, far1, sent1, result,
           far_send, far_recv, halo_send, halo_recv, load_sem, store_sem):
    me = lax.axis_index("seq")
    chunk, tile, near, halo, rows = plan.chunk, plan.tile, plan.near, plan.halo, plan.rows
    exts, fars = (ext0, ext1), (far0, far1)

    load = pltpu.make_async_copy(tokens.at[pl.ds(0, near), :], ext0.at[:, pl.ds(halo, rows)], load_sem)
    load.start()

    barrier = pltpu.get_barrier_semaphore()
    for peer in plan.peers:
        pl.semaphore_signal(barrier, inc=1, device_id={"seq": lax.rem(me + peer, plan.count)}, device_id_type=MESH)
    pl.semaphore_wait(barrier, len(plan.peers))

    def far_copy(block, index, number):
        cols = pl.ds(pl.multiple_of(number * chunk, LANES), chunk)
        if block == 0:
            source = tokens.at[pl.ds(near + index * TRACK_CH, TRACK_CH), cols]
        else:
            source = sent1.at[pl.ds(index * TRACK_CH, TRACK_CH), cols]
        return pltpu.make_async_remote_copy(
            src_ref=source,
            dst_ref=fars[block].at[pl.ds(index * TRACK_CH, TRACK_CH), cols],
            send_sem=far_send.at[block, index, number],
            recv_sem=far_recv.at[block, index, number],
            device_id={"seq": lax.rem(me + plan.distances[index], plan.count)},
            device_id_type=MESH,
        )

    def halo_copy(block, number):
        first, height, from_end, width, _, _ = plan.pieces[number]
        if block == 0:
            source = tokens.at[pl.ds(first, height), pl.ds(rows - from_end, width)]
        else:
            source = ext1.at[pl.ds(first, height), pl.ds(halo + rows - from_end, width)]
        return pltpu.make_async_remote_copy(
            src_ref=source,
            dst_ref=exts[block].at[pl.ds(first, height), pl.ds(halo - from_end, width)],
            send_sem=halo_send.at[block, number],
            recv_sem=halo_recv.at[block, number],
            device_id={"seq": lax.rem(me + 1, plan.count)},
            device_id_type=MESH,
        )

    def store(number):
        cols = pl.ds(pl.multiple_of(number * chunk, LANES), chunk)
        return pltpu.make_async_copy(result.at[:, cols], out.at[:, cols], store_sem.at[number])

    @pl.loop(0, plan.chunks)
    def _(step):
        number = plan.chunks - 1 - step
        for index in range(plan.far):
            far_copy(0, index, number).start()
        for piece, (*_, reader) in enumerate(plan.pieces):
            @pl.when(number == reader)
            def _(piece=piece):
                halo_copy(0, piece).start()

    load.wait()

    for block in range(BLOCKS):
        ext, far = exts[block], fars[block]

        @pl.loop(0, plan.chunks)
        def _(step, block=block, ext=ext, far=far):
            number = plan.chunks - 1 - step
            for index in range(plan.far):
                far_copy(block, index, number).wait_recv()
            for piece, (*_, reader) in enumerate(plan.pieces):
                @pl.when(number == reader)
                def _(piece=piece):
                    halo_copy(block, piece).wait_recv()

            @pl.loop(0, chunk // tile)
            def _(part):
                col = pl.multiple_of(number * chunk + part * tile, LANES)
                value = mix_tile(
                    rotated_tile(plan, ext, far, col),
                    gain[block], w_in[block], b_in[block], w_out[block], b_out[block],
                )
                if block + 1 < BLOCKS:
                    ext1[:, pl.ds(pl.multiple_of(halo + col, LANES), tile)] = value[:near]
                    sent1[:, pl.ds(col, tile)] = value[near:]
                else:
                    result[:, pl.ds(col, tile)] = value

            if block + 1 < BLOCKS:
                for index in range(plan.far):
                    far_copy(1, index, number).start()
                for piece, (*_, source, _) in enumerate(plan.pieces):
                    @pl.when(number == source)
                    def _(piece=piece):
                        halo_copy(1, piece).start()
            else:
                store(number).start()

    @pl.loop(0, plan.chunks)
    def _(number):
        for block in range(BLOCKS):
            for index in range(plan.far):
                far_copy(block, index, number).wait_send()
        store(number).wait()

    for block in range(BLOCKS):
        for piece in range(len(plan.pieces)):
            halo_copy(block, piece).wait_send()


def solution(mesh):
    count = mesh.shape["seq"]

    def shards(tokens, norm_gain, in_weight, in_bias, out_weight, out_bias):
        channels, rows = tokens.shape
        plan = Plan(count, rows, min(CHUNK, rows // 2), min(TILE, rows // 2))
        distant = plan.far * TRACK_CH
        wide = plan.halo + rows
        vmem = pl.BlockSpec(memory_space=pltpu.VMEM)
        return pl.pallas_call(
            functools.partial(kernel, plan),
            out_shape=jax.ShapeDtypeStruct(tokens.shape, tokens.dtype),
            in_specs=[pl.BlockSpec(memory_space=pl.ANY)] + [vmem] * 5,
            out_specs=pl.BlockSpec(memory_space=pl.ANY),
            scratch_shapes=[
                pltpu.VMEM((plan.near, wide), jnp.bfloat16),
                pltpu.VMEM((plan.near, wide), jnp.bfloat16),
                pltpu.VMEM((distant, rows), jnp.bfloat16),
                pltpu.VMEM((distant, rows), jnp.bfloat16),
                pltpu.VMEM((distant, rows), jnp.bfloat16),
                pltpu.VMEM((channels, rows), jnp.bfloat16),
                pltpu.SemaphoreType.DMA((BLOCKS, plan.far, plan.chunks)),
                pltpu.SemaphoreType.DMA((BLOCKS, plan.far, plan.chunks)),
                pltpu.SemaphoreType.DMA((BLOCKS, len(plan.pieces))),
                pltpu.SemaphoreType.DMA((BLOCKS, len(plan.pieces))),
                pltpu.SemaphoreType.DMA,
                pltpu.SemaphoreType.DMA((plan.chunks,)),
            ],
            compiler_params=pltpu.CompilerParams(
                collective_id=0, has_side_effects=True, vmem_limit_bytes=56 * 2**20
            ),
        )(tokens, norm_gain[:, :, None], in_weight, in_bias[:, :, None], out_weight, out_bias[:, :, None])

    return jax.shard_map(
        shards,
        mesh=mesh,
        in_specs=(P("batch", "seq"), P(), P(), P(), P(), P()),
        out_specs=P("batch", "seq"),
        check_vma=False,
    )
```

```python
import functools

import jax
import jax.numpy as jnp
from jax import lax
from jax.experimental import pallas as pl
from jax.experimental.pallas import tpu as pltpu
from jax.sharding import PartitionSpec as P

TRACK_CH = 16
TRACKS = 19
BLOCKS = 2
LANES = 128
CHUNK = 1024
TILE = 1024
LAG = 2
MESH = pl.DeviceIdType.MESH


class Plan:
    def __init__(self, count, rows, chunk, tile, plane):
        self.count, self.rows, self.chunk, self.tile = count, rows, chunk, tile
        self.chunks = rows // chunk
        self.short = 0
        while self.short + 1 < TRACKS and 2**self.short < rows:
            self.short += 1
        self.near = (1 + self.short) * TRACK_CH
        self.distances = [2 ** (t - 1) // rows for t in range(1 + self.short, TRACKS)]
        self.far = len(self.distances)
        self.halo = max(2 ** (self.short - 1), LANES)
        self.pieces = []
        small = sum(1 for t in range(1, 1 + self.short) if 2 ** (t - 1) < LANES)
        self.pieces.append((TRACK_CH, small * TRACK_CH, LANES, LANES, self.chunks - 1, 0))
        for t in range(1 + small, 1 + self.short):
            offset = 2 ** (t - 1)
            width = min(offset, chunk)
            for part in range(offset // width):
                from_end = offset - part * width
                source = (rows - from_end) // chunk
                self.pieces.append((t * TRACK_CH, TRACK_CH, from_end, width, source, part))
        self.plane = plane
        self.relays = []
        if plane:
            last = plane - 1
            self.relays = [(0, last, 2, 0), (None, last, 3, 0), (1, last - 1, 0, 0), (1, last, 1, 1)]
        peers = []
        hops = [1] + self.distances
        for _, sender, relay, receiver in self.relays:
            hops += [(relay - sender) % count, (plane + receiver - relay) % count]
        for d in hops:
            for signed in (d, count - d):
                if signed % count and signed % count not in peers:
                    peers.append(signed % count)
        self.peers = peers


def rotated_tile(plan, ext, far, col):
    tile, halo = plan.tile, plan.halo
    parts = []
    for t in range(1 + plan.short):
        rows = pl.ds(t * TRACK_CH, TRACK_CH)
        offset = 0 if t == 0 else 2 ** (t - 1)
        if offset % LANES == 0:
            start = pl.multiple_of(halo - offset + col, LANES)
            parts.append(ext[rows, pl.ds(start, tile)].astype(jnp.float32))
        else:
            start = pl.multiple_of(halo - LANES + col, LANES)
            window = ext[rows, pl.ds(start, tile + LANES)].astype(jnp.float32)
            parts.append(pltpu.roll(window, offset, 1)[:, LANES:])
    parts.append(far[:, pl.ds(pl.multiple_of(col, LANES), tile)].astype(jnp.float32))
    return jnp.concatenate(parts, 0)


def columns(row):
    return jnp.broadcast_to(row, (LANES, row.shape[1])).T


def across(column, width):
    return jnp.concatenate([column] * (width // LANES), 1)


def mix_tile(as_float, gain, in_weight, in_bias, out_weight, out_bias):
    mean_square = jnp.mean(as_float * as_float, axis=0, keepdims=True)
    normed = (as_float * gain * lax.rsqrt(mean_square + 1e-06)).astype(jnp.bfloat16)
    pre_act = jnp.dot(in_weight, normed, preferred_element_type=jnp.float32) + in_bias
    inner = pre_act * (0.7978845608028654 + 0.035677408136300125 * (pre_act * pre_act))
    half = 0.5 * pre_act
    active = (half + half * jnp.tanh(inner)).astype(jnp.bfloat16)
    summed = as_float + jnp.dot(out_weight, active, preferred_element_type=jnp.float32) + out_bias
    return summed.astype(jnp.bfloat16)


def kernel(plan, tokens, gain_in, w_in_t, b_in_in, w_out, b_out_in, out,
           gain, w_in, b_in, b_out, relay_far, relay_halo, ext0, ext1, far0, far1, sent1, result,
           far_send, far_recv, halo_send, halo_recv,
           pass_send, pass_recv, pass_halo_send, pass_halo_recv, load_sem, store_sem):
    me = lax.axis_index("seq")
    chunk, tile, near, halo, rows = plan.chunk, plan.tile, plan.near, plan.halo, plan.rows
    exts, fars = (ext0, ext1), (far0, far1)

    load = pltpu.make_async_copy(tokens.at[pl.ds(0, near), :], ext0.at[:, pl.ds(halo, rows)], load_sem)
    load.start()

    barrier = pltpu.get_barrier_semaphore()
    for peer in plan.peers:
        pl.semaphore_signal(barrier, inc=1, device_id={"seq": lax.rem(me + peer, plan.count)}, device_id_type=MESH)
    pl.semaphore_wait(barrier, len(plan.peers))

    place = lax.rem(me, plan.plane) if plan.plane else me

    def along(hop):
        return {"seq": lax.rem(me + hop + plan.count, plan.count)}

    def far_copy(block, index, number, relay=None):
        cols = pl.ds(pl.multiple_of(number * chunk, LANES), chunk)
        if block == 0:
            source = tokens.at[pl.ds(near + index * TRACK_CH, TRACK_CH), cols]
        else:
            source = sent1.at[pl.ds(index * TRACK_CH, TRACK_CH), cols]
        if relay is None:
            target = fars[block].at[pl.ds(index * TRACK_CH, TRACK_CH), cols]
            arrived, hop = far_recv.at[block, index, number], plan.distances[index]
        else:
            target, arrived, hop = relay_far.at[block, :, cols], pass_recv.at[block, number], relay[2] - relay[1]
        return pltpu.make_async_remote_copy(
            src_ref=source, dst_ref=target, send_sem=far_send.at[block, index, number], recv_sem=arrived,
            device_id=along(hop), device_id_type=MESH,
        )

    def far_pass(block, relay, number):
        index, _, at, receiver = relay
        cols = pl.ds(pl.multiple_of(number * chunk, LANES), chunk)
        return pltpu.make_async_remote_copy(
            src_ref=relay_far.at[block, :, cols],
            dst_ref=fars[block].at[pl.ds(index * TRACK_CH, TRACK_CH), cols],
            send_sem=pass_send.at[block, number],
            recv_sem=far_recv.at[block, index, number],
            device_id=along(plan.plane + receiver - at), device_id_type=MESH,
        )

    def halo_copy(block, number, relay=None):
        first, height, from_end, width, _, _ = plan.pieces[number]
        where = (pl.ds(first, height), pl.ds(halo - from_end, width))
        if block == 0:
            source = tokens.at[pl.ds(first, height), pl.ds(rows - from_end, width)]
        else:
            source = ext1.at[pl.ds(first, height), pl.ds(halo + rows - from_end, width)]
        if relay is None:
            target, arrived, hop = exts[block].at[where], halo_recv.at[block, number], 1
        else:
            target, arrived = relay_halo.at[(block, *where)], pass_halo_recv.at[block, number]
            hop = relay[2] - relay[1]
        return pltpu.make_async_remote_copy(
            src_ref=source, dst_ref=target, send_sem=halo_send.at[block, number], recv_sem=arrived,
            device_id=along(hop), device_id_type=MESH,
        )

    def halo_pass(block, relay, number):
        first, height, from_end, width, _, _ = plan.pieces[number]
        where = (pl.ds(first, height), pl.ds(halo - from_end, width))
        return pltpu.make_async_remote_copy(
            src_ref=relay_halo.at[(block, *where)],
            dst_ref=exts[block].at[where],
            send_sem=pass_halo_send.at[block, number],
            recv_sem=halo_recv.at[block, number],
            device_id=along(plan.plane + relay[3] - relay[2]), device_id_type=MESH,
        )

    def start(make, key, *args):
        relays = [relay for relay in plan.relays if relay[0] == key]
        direct = place >= 0
        for relay in relays:
            direct = direct & (place != relay[1])

            @pl.when(place == relay[1])
            def _(relay=relay):
                make(*args, relay=relay).start()

        if relays:
            @pl.when(direct)
            def _():
                make(*args).start()
        else:
            make(*args).start()

    def forward(block, number, halo_of):
        for relay in plan.relays:
            @pl.when((place == relay[2]) & (number >= 0) & (number < plan.chunks))
            def _(relay=relay):
                if relay[0] is None:
                    for piece in range(len(plan.pieces)):
                        @pl.when(number == plan.pieces[piece][halo_of])
                        def _(piece=piece):
                            halo_copy(block, piece, relay).wait_recv()
                            halo_pass(block, relay, piece).start()
                else:
                    far_copy(block, relay[0], number, relay).wait_recv()
                    far_pass(block, relay, number).start()

    def store(number):
        cols = pl.ds(pl.multiple_of(number * chunk, LANES), chunk)
        return pltpu.make_async_copy(result.at[:, cols], out.at[:, cols], store_sem.at[number])

    @pl.loop(0, plan.chunks)
    def _(step):
        number = plan.chunks - 1 - step
        for index in range(plan.far):
            start(far_copy, index, 0, index, number)
        for piece, (*_, reader) in enumerate(plan.pieces):
            @pl.when(number == reader)
            def _(piece=piece):
                start(halo_copy, None, 0, piece)

    forward(0, plan.chunks - 1, 5)

    for block in range(BLOCKS):
        gain[block] = columns(gain_in[block:block + 1, :])
        b_in[block] = columns(b_in_in[block:block + 1, :])
        b_out[block] = columns(b_out_in[block:block + 1, :])
        w_in[block] = w_in_t[block].T

    load.wait()

    for block in range(BLOCKS):
        ext, far = exts[block], fars[block]

        @pl.loop(0, plan.chunks)
        def _(step, block=block, ext=ext, far=far):
            number = plan.chunks - 1 - step
            if block == 0:
                forward(0, number - 1, 5)
            forward(1, number + LAG - block * plan.chunks, 4)
            for index in range(plan.far):
                far_copy(block, index, number).wait_recv()
            for piece, (*_, reader) in enumerate(plan.pieces):
                @pl.when(number == reader)
                def _(piece=piece):
                    halo_copy(block, piece).wait_recv()

            @pl.loop(0, chunk // tile)
            def _(part):
                col = pl.multiple_of(number * chunk + part * tile, LANES)
                value = mix_tile(
                    rotated_tile(plan, ext, far, col),
                    across(gain[block], tile), w_in[block], across(b_in[block], tile),
                    w_out[block], across(b_out[block], tile),
                )
                if block + 1 < BLOCKS:
                    ext1[:, pl.ds(pl.multiple_of(halo + col, LANES), tile)] = value[:near]
                    sent1[:, pl.ds(col, tile)] = value[near:]
                else:
                    result[:, pl.ds(col, tile)] = value

            if block + 1 < BLOCKS:
                for index in range(plan.far):
                    start(far_copy, index, 1, index, number)
                for piece, (*_, source, _) in enumerate(plan.pieces):
                    @pl.when(number == source)
                    def _(piece=piece):
                        start(halo_copy, None, 1, piece)
            else:
                store(number).start()

    @pl.loop(0, plan.chunks)
    def _(number):
        for block in range(BLOCKS):
            for index in range(plan.far):
                far_copy(block, index, number).wait_send()
            for relay in plan.relays:
                if relay[0] is not None:
                    @pl.when(place == relay[2])
                    def _(relay=relay, block=block):
                        far_pass(block, relay, number).wait_send()
        store(number).wait()

    for block in range(BLOCKS):
        for piece in range(len(plan.pieces)):
            halo_copy(block, piece).wait_send()
            for relay in plan.relays:
                if relay[0] is None:
                    @pl.when(place == relay[2])
                    def _(relay=relay, block=block, piece=piece):
                        halo_pass(block, relay, piece).wait_send()


def plane_of(mesh):
    devices = mesh.devices.reshape(-1)
    if mesh.shape["seq"] != devices.size or not hasattr(devices[0], "coords"):
        return 0
    places = [(*reversed(d.coords), d.core_on_chip) for d in devices]
    shape = tuple(max(p[axis] for p in places) + 1 for axis in range(4))
    plane = shape[1] * shape[2] * shape[3]
    ordered = [(i // plane, i // 4 % 2, i // 2 % 2, i % 2) for i in range(devices.size)]
    return plane if shape[1:] == (2, 2, 2) and shape[0] > 1 and places == ordered else 0


def solution(mesh):
    count = mesh.shape["seq"]
    plane = plane_of(mesh)

    def shards(tokens, norm_gain, in_weight, in_bias, out_weight, out_bias):
        channels, rows = tokens.shape
        plan = Plan(count, rows, min(CHUNK, rows // 2), min(TILE, rows // 2), plane)
        distant = plan.far * TRACK_CH
        wide = plan.halo + rows
        vmem = pl.BlockSpec(memory_space=pltpu.VMEM)
        return pl.pallas_call(
            functools.partial(kernel, plan),
            out_shape=jax.ShapeDtypeStruct(tokens.shape, tokens.dtype),
            in_specs=[pl.BlockSpec(memory_space=pl.ANY)] + [vmem] * 5,
            out_specs=pl.BlockSpec(memory_space=pl.ANY),
            scratch_shapes=[
                pltpu.VMEM((BLOCKS, channels, LANES), jnp.float32),
                pltpu.VMEM(in_weight.shape, jnp.bfloat16),
                pltpu.VMEM((BLOCKS, in_weight.shape[1], LANES), jnp.float32),
                pltpu.VMEM((BLOCKS, channels, LANES), jnp.float32),
                pltpu.VMEM((BLOCKS, TRACK_CH, rows), jnp.bfloat16),
                pltpu.VMEM((BLOCKS, plan.near, plan.halo), jnp.bfloat16),
                pltpu.VMEM((plan.near, wide), jnp.bfloat16),
                pltpu.VMEM((plan.near, wide), jnp.bfloat16),
                pltpu.VMEM((distant, rows), jnp.bfloat16),
                pltpu.VMEM((distant, rows), jnp.bfloat16),
                pltpu.VMEM((distant, rows), jnp.bfloat16),
                pltpu.VMEM((channels, rows), jnp.bfloat16),
                pltpu.SemaphoreType.DMA((BLOCKS, plan.far, plan.chunks)),
                pltpu.SemaphoreType.DMA((BLOCKS, plan.far, plan.chunks)),
                pltpu.SemaphoreType.DMA((BLOCKS, len(plan.pieces))),
                pltpu.SemaphoreType.DMA((BLOCKS, len(plan.pieces))),
                pltpu.SemaphoreType.DMA((BLOCKS, plan.chunks)),
                pltpu.SemaphoreType.DMA((BLOCKS, plan.chunks)),
                pltpu.SemaphoreType.DMA((BLOCKS, len(plan.pieces))),
                pltpu.SemaphoreType.DMA((BLOCKS, len(plan.pieces))),
                pltpu.SemaphoreType.DMA,
                pltpu.SemaphoreType.DMA((plan.chunks,)),
            ],
            compiler_params=pltpu.CompilerParams(
                collective_id=0, has_side_effects=True, vmem_limit_bytes=56 * 2**20
            ),
        )(tokens, norm_gain, jnp.swapaxes(in_weight, 1, 2), in_bias, out_weight, out_bias)

    return jax.shard_map(
        shards,
        mesh=mesh,
        in_specs=(P("batch", "seq"), P(), P(), P(), P(), P()),
        out_specs=P("batch", "seq"),
        check_vma=False,
    )
```

```python
import functools

import jax
import jax.numpy as jnp
from jax import lax
from jax.experimental import pallas as pl
from jax.experimental.pallas import tpu as pltpu
from jax.sharding import PartitionSpec as P

TRACK_CH = 16
TRACKS = 19
BLOCKS = 2
LANES = 128
CHUNK = 2048
TILE = 2048
LAG = 2
MESH = pl.DeviceIdType.MESH


class Plan:
    def __init__(self, count, rows, chunk, tile, plane):
        self.count, self.rows, self.chunk, self.tile = count, rows, chunk, tile
        self.chunks = rows // chunk
        self.short = 0
        while self.short + 1 < TRACKS and 2**self.short < rows:
            self.short += 1
        self.near = (1 + self.short) * TRACK_CH
        self.distances = [2 ** (t - 1) // rows for t in range(1 + self.short, TRACKS)]
        self.far = len(self.distances)
        self.halo = max(2 ** (self.short - 1), LANES)
        self.pieces = []
        small = sum(1 for t in range(1, 1 + self.short) if 2 ** (t - 1) < LANES)
        self.pieces.append((TRACK_CH, small * TRACK_CH, LANES, LANES, self.chunks - 1, 0))
        for t in range(1 + small, 1 + self.short):
            offset = 2 ** (t - 1)
            width = min(offset, chunk)
            for part in range(offset // width):
                from_end = offset - part * width
                source = (rows - from_end) // chunk
                self.pieces.append((t * TRACK_CH, TRACK_CH, from_end, width, source, part))
        self.plane = plane
        self.relays = []
        if plane:
            last = plane - 1
            self.relays = [(0, last, 2, 0), (None, last, 3, 0), (1, last - 1, 0, 0), (1, last, 1, 1)]
        peers = []
        hops = [1] + self.distances
        for _, sender, relay, receiver in self.relays:
            hops += [(relay - sender) % count, (plane + receiver - relay) % count]
        for d in hops:
            for signed in (d, count - d):
                if signed % count and signed % count not in peers:
                    peers.append(signed % count)
        self.peers = peers


def rotated_tile(plan, ext, far, col):
    tile, halo = plan.tile, plan.halo
    parts = []
    for t in range(1 + plan.short):
        rows = pl.ds(t * TRACK_CH, TRACK_CH)
        offset = 0 if t == 0 else 2 ** (t - 1)
        if offset % LANES == 0:
            start = pl.multiple_of(halo - offset + col, LANES)
            parts.append(ext[rows, pl.ds(start, tile)].astype(jnp.float32))
        else:
            start = pl.multiple_of(halo - LANES + col, LANES)
            window = ext[rows, pl.ds(start, tile + LANES)].astype(jnp.float32)
            parts.append(pltpu.roll(window, offset, 1)[:, LANES:])
    parts.append(far[:, pl.ds(pl.multiple_of(col, LANES), tile)].astype(jnp.float32))
    return jnp.concatenate(parts, 0)


def columns(row):
    return jnp.broadcast_to(row, (LANES, row.shape[1])).T


def across(column, width):
    return jnp.concatenate([column] * (width // LANES), 1)


def mix_tile(as_float, gain, in_weight, in_bias, out_weight, out_bias):
    mean_square = jnp.mean(as_float * as_float, axis=0, keepdims=True)
    normed = (as_float * gain * lax.rsqrt(mean_square + 1e-06)).astype(jnp.bfloat16)
    pre_act = jnp.dot(in_weight, normed, preferred_element_type=jnp.float32) + in_bias
    inner = pre_act * (0.7978845608028654 + 0.035677408136300125 * (pre_act * pre_act))
    half = 0.5 * pre_act
    active = (half + half * jnp.tanh(inner)).astype(jnp.bfloat16)
    summed = as_float + jnp.dot(out_weight, active, preferred_element_type=jnp.float32) + out_bias
    return summed.astype(jnp.bfloat16)


def kernel(plan, tokens, gain_in, w_in_t, b_in_in, w_out, b_out_in, out,
           gain, w_in, b_in, b_out, relay_far, relay_halo, ext0, ext1, far0, far1, sent1, result,
           far_send, far_recv, halo_send, halo_recv,
           pass_send, pass_recv, pass_halo_send, pass_halo_recv, load_sem, store_sem):
    me = lax.axis_index("seq")
    chunk, tile, near, halo, rows = plan.chunk, plan.tile, plan.near, plan.halo, plan.rows
    exts, fars = (ext0, ext1), (far0, far1)

    load = pltpu.make_async_copy(tokens.at[pl.ds(0, near), :], ext0.at[:, pl.ds(halo, rows)], load_sem)
    load.start()

    barrier = pltpu.get_barrier_semaphore()
    for peer in plan.peers:
        pl.semaphore_signal(barrier, inc=1, device_id={"seq": lax.rem(me + peer, plan.count)}, device_id_type=MESH)
    pl.semaphore_wait(barrier, len(plan.peers))

    place = lax.rem(me, plan.plane) if plan.plane else me

    def along(hop):
        return {"seq": lax.rem(me + hop + plan.count, plan.count)}

    def far_copy(block, index, number, relay=None):
        cols = pl.ds(pl.multiple_of(number * chunk, LANES), chunk)
        if block == 0:
            source = tokens.at[pl.ds(near + index * TRACK_CH, TRACK_CH), cols]
        else:
            source = sent1.at[pl.ds(index * TRACK_CH, TRACK_CH), cols]
        if relay is None:
            target = fars[block].at[pl.ds(index * TRACK_CH, TRACK_CH), cols]
            arrived, hop = far_recv.at[block, index, number], plan.distances[index]
        else:
            target, arrived, hop = relay_far.at[block, :, cols], pass_recv.at[block, number], relay[2] - relay[1]
        return pltpu.make_async_remote_copy(
            src_ref=source, dst_ref=target, send_sem=far_send.at[block, index, number], recv_sem=arrived,
            device_id=along(hop), device_id_type=MESH,
        )

    def far_pass(block, relay, number):
        index, _, at, receiver = relay
        cols = pl.ds(pl.multiple_of(number * chunk, LANES), chunk)
        return pltpu.make_async_remote_copy(
            src_ref=relay_far.at[block, :, cols],
            dst_ref=fars[block].at[pl.ds(index * TRACK_CH, TRACK_CH), cols],
            send_sem=pass_send.at[block, number],
            recv_sem=far_recv.at[block, index, number],
            device_id=along(plan.plane + receiver - at), device_id_type=MESH,
        )

    def halo_copy(block, number, relay=None):
        first, height, from_end, width, _, _ = plan.pieces[number]
        where = (pl.ds(first, height), pl.ds(halo - from_end, width))
        if block == 0:
            source = tokens.at[pl.ds(first, height), pl.ds(rows - from_end, width)]
        else:
            source = ext1.at[pl.ds(first, height), pl.ds(halo + rows - from_end, width)]
        if relay is None:
            target, arrived, hop = exts[block].at[where], halo_recv.at[block, number], 1
        else:
            target, arrived = relay_halo.at[(block, *where)], pass_halo_recv.at[block, number]
            hop = relay[2] - relay[1]
        return pltpu.make_async_remote_copy(
            src_ref=source, dst_ref=target, send_sem=halo_send.at[block, number], recv_sem=arrived,
            device_id=along(hop), device_id_type=MESH,
        )

    def halo_pass(block, relay, number):
        first, height, from_end, width, _, _ = plan.pieces[number]
        where = (pl.ds(first, height), pl.ds(halo - from_end, width))
        return pltpu.make_async_remote_copy(
            src_ref=relay_halo.at[(block, *where)],
            dst_ref=exts[block].at[where],
            send_sem=pass_halo_send.at[block, number],
            recv_sem=halo_recv.at[block, number],
            device_id=along(plan.plane + relay[3] - relay[2]), device_id_type=MESH,
        )

    def start(make, key, *args):
        relays = [relay for relay in plan.relays if relay[0] == key]
        direct = place >= 0
        for relay in relays:
            direct = direct & (place != relay[1])

            @pl.when(place == relay[1])
            def _(relay=relay):
                make(*args, relay=relay).start()

        if relays:
            @pl.when(direct)
            def _():
                make(*args).start()
        else:
            make(*args).start()

    def forward(block, number, halo_of):
        for relay in plan.relays:
            @pl.when((place == relay[2]) & (number >= 0) & (number < plan.chunks))
            def _(relay=relay):
                if relay[0] is None:
                    for piece in range(len(plan.pieces)):
                        @pl.when(number == plan.pieces[piece][halo_of])
                        def _(piece=piece):
                            halo_copy(block, piece, relay).wait_recv()
                            halo_pass(block, relay, piece).start()
                else:
                    far_copy(block, relay[0], number, relay).wait_recv()
                    far_pass(block, relay, number).start()

    def store(number):
        cols = pl.ds(pl.multiple_of(number * chunk, LANES), chunk)
        return pltpu.make_async_copy(result.at[:, cols], out.at[:, cols], store_sem.at[number])

    @pl.loop(0, plan.chunks)
    def _(step):
        number = plan.chunks - 1 - step
        for index in range(plan.far):
            start(far_copy, index, 0, index, number)
        for piece, (*_, reader) in enumerate(plan.pieces):
            @pl.when(number == reader)
            def _(piece=piece):
                start(halo_copy, None, 0, piece)

    forward(0, plan.chunks - 1, 5)

    for block in range(BLOCKS):
        gain[block] = columns(gain_in[block:block + 1, :])
        b_in[block] = columns(b_in_in[block:block + 1, :])
        b_out[block] = columns(b_out_in[block:block + 1, :])
        w_in[block] = w_in_t[block].T

    load.wait()

    for block in range(BLOCKS):
        ext, far = exts[block], fars[block]

        @pl.loop(0, plan.chunks)
        def _(step, block=block, ext=ext, far=far):
            number = plan.chunks - 1 - step
            if block == 0:
                forward(0, number - 1, 5)
            forward(1, number + LAG - block * plan.chunks, 4)
            for index in range(plan.far):
                far_copy(block, index, number).wait_recv()
            for piece, (*_, reader) in enumerate(plan.pieces):
                @pl.when(number == reader)
                def _(piece=piece):
                    halo_copy(block, piece).wait_recv()

            @pl.loop(0, chunk // tile)
            def _(part):
                col = pl.multiple_of(number * chunk + part * tile, LANES)
                value = mix_tile(
                    rotated_tile(plan, ext, far, col),
                    across(gain[block], tile), w_in[block], across(b_in[block], tile),
                    w_out[block], across(b_out[block], tile),
                )
                if block + 1 < BLOCKS:
                    ext1[:, pl.ds(pl.multiple_of(halo + col, LANES), tile)] = value[:near]
                    sent1[:, pl.ds(col, tile)] = value[near:]
                else:
                    result[:, pl.ds(col, tile)] = value

            if block + 1 < BLOCKS:
                for index in range(plan.far):
                    start(far_copy, index, 1, index, number)
                for piece, (*_, source, _) in enumerate(plan.pieces):
                    @pl.when(number == source)
                    def _(piece=piece):
                        start(halo_copy, None, 1, piece)
            else:
                store(number).start()

    @pl.loop(0, plan.chunks)
    def _(number):
        for block in range(BLOCKS):
            for index in range(plan.far):
                far_copy(block, index, number).wait_send()
            for relay in plan.relays:
                if relay[0] is not None:
                    @pl.when(place == relay[2])
                    def _(relay=relay, block=block):
                        far_pass(block, relay, number).wait_send()
        store(number).wait()

    for block in range(BLOCKS):
        for piece in range(len(plan.pieces)):
            halo_copy(block, piece).wait_send()
            for relay in plan.relays:
                if relay[0] is None:
                    @pl.when(place == relay[2])
                    def _(relay=relay, block=block, piece=piece):
                        halo_pass(block, relay, piece).wait_send()


def plane_of(mesh):
    devices = mesh.devices.reshape(-1)
    if mesh.shape["seq"] != devices.size or not hasattr(devices[0], "coords"):
        return 0
    places = [(*reversed(d.coords), d.core_on_chip) for d in devices]
    shape = tuple(max(p[axis] for p in places) + 1 for axis in range(4))
    plane = shape[1] * shape[2] * shape[3]
    ordered = [(i // plane, i // 4 % 2, i // 2 % 2, i % 2) for i in range(devices.size)]
    return plane if shape[1:] == (2, 2, 2) and shape[0] > 1 and places == ordered else 0


def solution(mesh):
    count = mesh.shape["seq"]
    plane = plane_of(mesh)

    def shards(tokens, norm_gain, in_weight, in_bias, out_weight, out_bias):
        channels, rows = tokens.shape
        plan = Plan(count, rows, min(CHUNK, rows // 2), min(TILE, rows // 2), plane)
        distant = plan.far * TRACK_CH
        wide = plan.halo + rows
        vmem = pl.BlockSpec(memory_space=pltpu.VMEM)
        return pl.pallas_call(
            functools.partial(kernel, plan),
            out_shape=jax.ShapeDtypeStruct(tokens.shape, tokens.dtype),
            in_specs=[pl.BlockSpec(memory_space=pl.ANY)] + [vmem] * 5,
            out_specs=pl.BlockSpec(memory_space=pl.ANY),
            scratch_shapes=[
                pltpu.VMEM((BLOCKS, channels, LANES), jnp.float32),
                pltpu.VMEM(in_weight.shape, jnp.bfloat16),
                pltpu.VMEM((BLOCKS, in_weight.shape[1], LANES), jnp.float32),
                pltpu.VMEM((BLOCKS, channels, LANES), jnp.float32),
                pltpu.VMEM((BLOCKS, TRACK_CH, rows), jnp.bfloat16),
                pltpu.VMEM((BLOCKS, plan.near, plan.halo), jnp.bfloat16),
                pltpu.VMEM((plan.near, wide), jnp.bfloat16),
                pltpu.VMEM((plan.near, wide), jnp.bfloat16),
                pltpu.VMEM((distant, rows), jnp.bfloat16),
                pltpu.VMEM((distant, rows), jnp.bfloat16),
                pltpu.VMEM((distant, rows), jnp.bfloat16),
                pltpu.VMEM((channels, rows), jnp.bfloat16),
                pltpu.SemaphoreType.DMA((BLOCKS, plan.far, plan.chunks)),
                pltpu.SemaphoreType.DMA((BLOCKS, plan.far, plan.chunks)),
                pltpu.SemaphoreType.DMA((BLOCKS, len(plan.pieces))),
                pltpu.SemaphoreType.DMA((BLOCKS, len(plan.pieces))),
                pltpu.SemaphoreType.DMA((BLOCKS, plan.chunks)),
                pltpu.SemaphoreType.DMA((BLOCKS, plan.chunks)),
                pltpu.SemaphoreType.DMA((BLOCKS, len(plan.pieces))),
                pltpu.SemaphoreType.DMA((BLOCKS, len(plan.pieces))),
                pltpu.SemaphoreType.DMA,
                pltpu.SemaphoreType.DMA((plan.chunks,)),
            ],
            compiler_params=pltpu.CompilerParams(
                collective_id=0, has_side_effects=True, vmem_limit_bytes=56 * 2**20
            ),
        )(tokens, norm_gain, jnp.swapaxes(in_weight, 1, 2), in_bias, out_weight, out_bias)

    return jax.shard_map(
        shards,
        mesh=mesh,
        in_specs=(P("batch", "seq"), P(), P(), P(), P(), P()),
        out_specs=P("batch", "seq"),
        check_vma=False,
    )
```

```python
import functools

import jax
import jax.numpy as jnp
from jax import lax
from jax.experimental import pallas as pl
from jax.experimental.pallas import tpu as pltpu
from jax.sharding import PartitionSpec as P

TRACK_CH = 16
TRACKS = 19
BLOCKS = 2
LANES = 128
CHUNK = 2048
TILE = 2048
LAG = 3
MESH = pl.DeviceIdType.MESH


class Plan:
    def __init__(self, count, rows, chunk, tile, plane):
        self.count, self.rows, self.chunk, self.tile = count, rows, chunk, tile
        self.chunks = rows // chunk
        self.short = 0
        while self.short + 1 < TRACKS and 2**self.short < rows:
            self.short += 1
        self.near = (1 + self.short) * TRACK_CH
        self.distances = [2 ** (t - 1) // rows for t in range(1 + self.short, TRACKS)]
        self.far = len(self.distances)
        self.halo = max(2 ** (self.short - 1), LANES)
        self.pieces = []
        small = sum(1 for t in range(1, 1 + self.short) if 2 ** (t - 1) < LANES)
        self.pieces.append((TRACK_CH, small * TRACK_CH, LANES, LANES, self.chunks - 1, 0))
        for t in range(1 + small, 1 + self.short):
            offset = 2 ** (t - 1)
            width = min(offset, chunk)
            for part in range(offset // width):
                from_end = offset - part * width
                source = (rows - from_end) // chunk
                self.pieces.append((t * TRACK_CH, TRACK_CH, from_end, width, source, part))
        self.plane = plane
        self.relays = []
        if plane:
            last = plane - 1
            self.relays = [(0, last, 2, 0), (None, last, 3, 0), (1, last - 1, 0, 0), (1, last, 1, 1)]
        peers = []
        hops = [1] + self.distances
        for _, sender, relay, receiver in self.relays:
            hops += [(relay - sender) % count, (plane + receiver - relay) % count]
        for d in hops:
            for signed in (d, count - d):
                if signed % count and signed % count not in peers:
                    peers.append(signed % count)
        self.peers = peers


def rotated_tile(plan, ext, far, col):
    tile, halo = plan.tile, plan.halo
    parts = []
    for t in range(1 + plan.short):
        rows = pl.ds(t * TRACK_CH, TRACK_CH)
        offset = 0 if t == 0 else 2 ** (t - 1)
        if offset % LANES == 0:
            start = pl.multiple_of(halo - offset + col, LANES)
            parts.append(ext[rows, pl.ds(start, tile)].astype(jnp.float32))
        else:
            start = pl.multiple_of(halo - LANES + col, LANES)
            window = ext[rows, pl.ds(start, tile + LANES)].astype(jnp.float32)
            parts.append(pltpu.roll(window, offset, 1)[:, LANES:])
    parts.append(far[:, pl.ds(pl.multiple_of(col, LANES), tile)].astype(jnp.float32))
    return jnp.concatenate(parts, 0)


def columns(row):
    return jnp.broadcast_to(row, (LANES, row.shape[1])).T


def across(column, width):
    return jnp.concatenate([column] * (width // LANES), 1)


def mix_tile(as_float, gain, in_weight, in_bias, out_weight, out_bias):
    mean_square = jnp.mean(as_float * as_float, axis=0, keepdims=True)
    normed = (as_float * gain * lax.rsqrt(mean_square + 1e-06)).astype(jnp.bfloat16)
    pre_act = jnp.dot(in_weight, normed, preferred_element_type=jnp.float32) + in_bias
    inner = pre_act * (0.7978845608028654 + 0.035677408136300125 * (pre_act * pre_act))
    half = 0.5 * pre_act
    active = (half + half * jnp.tanh(inner)).astype(jnp.bfloat16)
    summed = as_float + jnp.dot(out_weight, active, preferred_element_type=jnp.float32) + out_bias
    return summed.astype(jnp.bfloat16)


def kernel(plan, tokens, gain_in, w_in_t, b_in_in, w_out, b_out_in, out,
           gain, w_in, b_in, b_out, relay_far, relay_halo, ext0, ext1, far0, far1, sent1, result,
           far_send, far_recv, halo_send, halo_recv,
           pass_send, pass_recv, pass_halo_send, pass_halo_recv, load_sem, store_sem):
    me = lax.axis_index("seq")
    chunk, tile, near, halo, rows = plan.chunk, plan.tile, plan.near, plan.halo, plan.rows
    exts, fars = (ext0, ext1), (far0, far1)

    load = pltpu.make_async_copy(tokens.at[pl.ds(0, near), :], ext0.at[:, pl.ds(halo, rows)], load_sem)
    load.start()

    barrier = pltpu.get_barrier_semaphore()
    for peer in plan.peers:
        pl.semaphore_signal(barrier, inc=1, device_id={"seq": lax.rem(me + peer, plan.count)}, device_id_type=MESH)
    pl.semaphore_wait(barrier, len(plan.peers))

    place = lax.rem(me, plan.plane) if plan.plane else me

    def along(hop):
        return {"seq": lax.rem(me + hop + plan.count, plan.count)}

    def far_copy(block, index, number, relay=None):
        cols = pl.ds(pl.multiple_of(number * chunk, LANES), chunk)
        if block == 0:
            source = tokens.at[pl.ds(near + index * TRACK_CH, TRACK_CH), cols]
        else:
            source = sent1.at[pl.ds(index * TRACK_CH, TRACK_CH), cols]
        if relay is None:
            target = fars[block].at[pl.ds(index * TRACK_CH, TRACK_CH), cols]
            arrived, hop = far_recv.at[block, index, number], plan.distances[index]
        else:
            target, arrived, hop = relay_far.at[block, :, cols], pass_recv.at[block, number], relay[2] - relay[1]
        return pltpu.make_async_remote_copy(
            src_ref=source, dst_ref=target, send_sem=far_send.at[block, index, number], recv_sem=arrived,
            device_id=along(hop), device_id_type=MESH,
        )

    def far_pass(block, relay, number):
        index, _, at, receiver = relay
        cols = pl.ds(pl.multiple_of(number * chunk, LANES), chunk)
        return pltpu.make_async_remote_copy(
            src_ref=relay_far.at[block, :, cols],
            dst_ref=fars[block].at[pl.ds(index * TRACK_CH, TRACK_CH), cols],
            send_sem=pass_send.at[block, number],
            recv_sem=far_recv.at[block, index, number],
            device_id=along(plan.plane + receiver - at), device_id_type=MESH,
        )

    def halo_copy(block, number, relay=None):
        first, height, from_end, width, _, _ = plan.pieces[number]
        where = (pl.ds(first, height), pl.ds(halo - from_end, width))
        if block == 0:
            source = tokens.at[pl.ds(first, height), pl.ds(rows - from_end, width)]
        else:
            source = ext1.at[pl.ds(first, height), pl.ds(halo + rows - from_end, width)]
        if relay is None:
            target, arrived, hop = exts[block].at[where], halo_recv.at[block, number], 1
        else:
            target, arrived = relay_halo.at[(block, *where)], pass_halo_recv.at[block, number]
            hop = relay[2] - relay[1]
        return pltpu.make_async_remote_copy(
            src_ref=source, dst_ref=target, send_sem=halo_send.at[block, number], recv_sem=arrived,
            device_id=along(hop), device_id_type=MESH,
        )

    def halo_pass(block, relay, number):
        first, height, from_end, width, _, _ = plan.pieces[number]
        where = (pl.ds(first, height), pl.ds(halo - from_end, width))
        return pltpu.make_async_remote_copy(
            src_ref=relay_halo.at[(block, *where)],
            dst_ref=exts[block].at[where],
            send_sem=pass_halo_send.at[block, number],
            recv_sem=halo_recv.at[block, number],
            device_id=along(plan.plane + relay[3] - relay[2]), device_id_type=MESH,
        )

    def start(make, key, *args):
        relays = [relay for relay in plan.relays if relay[0] == key]
        direct = place >= 0
        for relay in relays:
            direct = direct & (place != relay[1])

            @pl.when(place == relay[1])
            def _(relay=relay):
                make(*args, relay=relay).start()

        if relays:
            @pl.when(direct)
            def _():
                make(*args).start()
        else:
            make(*args).start()

    def forward(block, number, halo_of):
        for relay in plan.relays:
            @pl.when((place == relay[2]) & (number >= 0) & (number < plan.chunks))
            def _(relay=relay):
                if relay[0] is None:
                    for piece in range(len(plan.pieces)):
                        @pl.when(number == plan.pieces[piece][halo_of])
                        def _(piece=piece):
                            halo_copy(block, piece, relay).wait_recv()
                            halo_pass(block, relay, piece).start()
                else:
                    far_copy(block, relay[0], number, relay).wait_recv()
                    far_pass(block, relay, number).start()

    def store(number):
        cols = pl.ds(pl.multiple_of(number * chunk, LANES), chunk)
        return pltpu.make_async_copy(result.at[:, cols], out.at[:, cols], store_sem.at[number])

    @pl.loop(0, plan.chunks)
    def _(step):
        number = plan.chunks - 1 - step
        for index in range(plan.far):
            start(far_copy, index, 0, index, number)
        for piece, (*_, reader) in enumerate(plan.pieces):
            @pl.when(number == reader)
            def _(piece=piece):
                start(halo_copy, None, 0, piece)

    forward(0, plan.chunks - 1, 5)

    for block in range(BLOCKS):
        gain[block] = columns(gain_in[block:block + 1, :])
        b_in[block] = columns(b_in_in[block:block + 1, :])
        b_out[block] = columns(b_out_in[block:block + 1, :])
        w_in[block] = w_in_t[block].T

    load.wait()

    for block in range(BLOCKS):
        ext, far = exts[block], fars[block]

        @pl.loop(0, plan.chunks)
        def _(step, block=block, ext=ext, far=far):
            number = plan.chunks - 1 - step
            if block == 0:
                forward(0, number - 1, 5)
            forward(1, number + LAG - block * plan.chunks, 4)
            for index in range(plan.far):
                far_copy(block, index, number).wait_recv()
            for piece, (*_, reader) in enumerate(plan.pieces):
                @pl.when(number == reader)
                def _(piece=piece):
                    halo_copy(block, piece).wait_recv()

            @pl.loop(0, chunk // tile)
            def _(part):
                col = pl.multiple_of(number * chunk + part * tile, LANES)
                value = mix_tile(
                    rotated_tile(plan, ext, far, col),
                    across(gain[block], tile), w_in[block], across(b_in[block], tile),
                    w_out[block], across(b_out[block], tile),
                )
                if block + 1 < BLOCKS:
                    ext1[:, pl.ds(pl.multiple_of(halo + col, LANES), tile)] = value[:near]
                    sent1[:, pl.ds(col, tile)] = value[near:]
                else:
                    result[:, pl.ds(col, tile)] = value

            if block + 1 < BLOCKS:
                for index in range(plan.far):
                    start(far_copy, index, 1, index, number)
                for piece, (*_, source, _) in enumerate(plan.pieces):
                    @pl.when(number == source)
                    def _(piece=piece):
                        start(halo_copy, None, 1, piece)
            else:
                store(number).start()

    @pl.loop(0, plan.chunks)
    def _(number):
        for block in range(BLOCKS):
            for index in range(plan.far):
                far_copy(block, index, number).wait_send()
            for relay in plan.relays:
                if relay[0] is not None:
                    @pl.when(place == relay[2])
                    def _(relay=relay, block=block):
                        far_pass(block, relay, number).wait_send()
        store(number).wait()

    for block in range(BLOCKS):
        for piece in range(len(plan.pieces)):
            halo_copy(block, piece).wait_send()
            for relay in plan.relays:
                if relay[0] is None:
                    @pl.when(place == relay[2])
                    def _(relay=relay, block=block, piece=piece):
                        halo_pass(block, relay, piece).wait_send()


def plane_of(mesh):
    devices = mesh.devices.reshape(-1)
    if mesh.shape["seq"] != devices.size or not hasattr(devices[0], "coords"):
        return 0
    places = [(*reversed(d.coords), d.core_on_chip) for d in devices]
    shape = tuple(max(p[axis] for p in places) + 1 for axis in range(4))
    plane = shape[1] * shape[2] * shape[3]
    ordered = [(i // plane, i // 4 % 2, i // 2 % 2, i % 2) for i in range(devices.size)]
    return plane if shape[1:] == (2, 2, 2) and shape[0] > 1 and places == ordered else 0


def solution(mesh):
    count = mesh.shape["seq"]
    plane = plane_of(mesh)

    def shards(tokens, norm_gain, in_weight, in_bias, out_weight, out_bias):
        channels, rows = tokens.shape
        plan = Plan(count, rows, min(CHUNK, rows // 2), min(TILE, rows // 2), plane)
        distant = plan.far * TRACK_CH
        wide = plan.halo + rows
        vmem = pl.BlockSpec(memory_space=pltpu.VMEM)
        return pl.pallas_call(
            functools.partial(kernel, plan),
            out_shape=jax.ShapeDtypeStruct(tokens.shape, tokens.dtype),
            in_specs=[pl.BlockSpec(memory_space=pl.ANY)] + [vmem] * 5,
            out_specs=pl.BlockSpec(memory_space=pl.ANY),
            scratch_shapes=[
                pltpu.VMEM((BLOCKS, channels, LANES), jnp.float32),
                pltpu.VMEM(in_weight.shape, jnp.bfloat16),
                pltpu.VMEM((BLOCKS, in_weight.shape[1], LANES), jnp.float32),
                pltpu.VMEM((BLOCKS, channels, LANES), jnp.float32),
                pltpu.VMEM((BLOCKS, TRACK_CH, rows), jnp.bfloat16),
                pltpu.VMEM((BLOCKS, plan.near, plan.halo), jnp.bfloat16),
                pltpu.VMEM((plan.near, wide), jnp.bfloat16),
                pltpu.VMEM((plan.near, wide), jnp.bfloat16),
                pltpu.VMEM((distant, rows), jnp.bfloat16),
                pltpu.VMEM((distant, rows), jnp.bfloat16),
                pltpu.VMEM((distant, rows), jnp.bfloat16),
                pltpu.VMEM((channels, rows), jnp.bfloat16),
                pltpu.SemaphoreType.DMA((BLOCKS, plan.far, plan.chunks)),
                pltpu.SemaphoreType.DMA((BLOCKS, plan.far, plan.chunks)),
                pltpu.SemaphoreType.DMA((BLOCKS, len(plan.pieces))),
                pltpu.SemaphoreType.DMA((BLOCKS, len(plan.pieces))),
                pltpu.SemaphoreType.DMA((BLOCKS, plan.chunks)),
                pltpu.SemaphoreType.DMA((BLOCKS, plan.chunks)),
                pltpu.SemaphoreType.DMA((BLOCKS, len(plan.pieces))),
                pltpu.SemaphoreType.DMA((BLOCKS, len(plan.pieces))),
                pltpu.SemaphoreType.DMA,
                pltpu.SemaphoreType.DMA((plan.chunks,)),
            ],
            compiler_params=pltpu.CompilerParams(
                collective_id=0, has_side_effects=True, vmem_limit_bytes=56 * 2**20
            ),
        )(tokens, norm_gain, jnp.swapaxes(in_weight, 1, 2), in_bias, out_weight, out_bias)

    return jax.shard_map(
        shards,
        mesh=mesh,
        in_specs=(P("batch", "seq"), P(), P(), P(), P(), P()),
        out_specs=P("batch", "seq"),
        check_vma=False,
    )
```
